128 devices in a mesh: region: 16 (over y, x), tile: 8 (over z, core).
Axes of the slice: x: 4, y: 4, z: 4, core: 2. Of those that a mesh axis runs over, the one named last changes fastest.
Arguments:
- state: float32 [80, 8, 32768], P(None, 'tile', 'region'), may hold values from -6 to 6
- obs_rows: float32 [16, 80, 8, 128], P('region', None, 'tile'), may hold values from -6 to 6
- obs_value: float32 [16, 8, 128], P('region', 'tile'), may hold values from -6 to 6
- obs_noise: float32 [16, 8, 128], P('region', 'tile'), may hold values from 0.3 to 3
- obs_cell: int32 [16, 8, 128], P('region', 'tile'), may hold values from 0 to 32767
- obs_class: int32 [16, 8, 128], P('region', 'tile'), may hold values from 0 to 2
- obs_count: int32 [16, 8], P('region', 'tile'), may hold values from 1 to 128, 512 in all within a row
Outputs:
- posterior: float32 [80, 8, 32768], P(None, 'tile', 'region')
The draws below stay inside these ranges and needn't reach their ends.
Inputs may be any that keep to these rules, and one draw needn't show every extreme that they name: `obs_count`: in every batch some tile has exactly 128 live slots.
All inputs are finite; a program needn't handle non-finite values. No bound on the sum of `obs_count` on one device may be relied on, other than what follows from the above.
Results may differ from the reference program's by a relative error of at most 0.0003.
Values sent between devices are 32-bit elements; how exact they have to be, the bound alone decides.
No kernel may reach another device: no remote copies, remote signals or barrier semaphores. Data moves between devices by JAX's collectives and lax.ppermute only.
A program may use at most 64 MiB of HBM per device.

```python
import math
import jax
import jax.numpy as jnp
import numpy as np
from jax import lax

M = 80
K_DEV = 128
TILES = 8
BATCHES = 16
TILE_CELLS = 32768


def place_ends(array, rng, smallest, largest):
    longest = array.shape.index(max(array.shape))
    spots = []
    for shift in (0, 1):
        where = [jax.random.randint(jax.random.fold_in(rng, axis), (), 0, length) for axis, length in enumerate(array.shape)]
        where[longest] = (where[longest] + shift) % array.shape[longest]
        spots.append(tuple(where))
    return array.at[spots[0]].set(smallest).at[spots[1]].set(largest)


def shard_levels(stream_key, dims, pieces, least, top_value):
    loudness = 1.0
    for axis_at, blocks in pieces:
        steps = jax.random.uniform(jax.random.fold_in(jax.random.fold_in(stream_key, 6), axis_at), (blocks,), jnp.float32, least / len(pieces), top_value / len(pieces))
        loudness = loudness * jnp.repeat(jnp.exp(steps), dims[axis_at] // blocks).reshape((-1,) + (1,) * (len(dims) - 1 - axis_at))
    return loudness


def profile(number_of, total, reach, skew):
    weights = [(1 << 20) // math.isqrt(rank ** skew) + 1 for rank in range(2, number_of + 1)]
    rest, holding = total - reach - (number_of - 1), [1] * (number_of - 1)
    while rest > 0:
        candidates = [i for i in range(number_of - 1) if holding[i] < reach]
        pool, left = sum([weights[i] for i in candidates]), rest
        for i in candidates:
            extra = min(reach - holding[i], max(1, left * weights[i] // pool), rest)
            holding[i] = holding[i] + extra
            rest = rest - extra
    return np.array([reach] + holding)


def uneven(own_key, number_of, total, most, slope):
    if number_of == 2:
        one = jax.random.randint(own_key, (), max(1, total - most), min(most, total - 1) + 1)
        return jnp.stack([one, total - one])
    sizes = jnp.asarray(profile(number_of, total, most, slope), jnp.int32)
    couples = (number_of - 1) // 2
    source_of, sink = sizes[1:1 + 2 * couples:2], sizes[2:2 + 2 * couples:2]
    room = jnp.minimum(source_of - 1, most - sink)
    shifted = jax.random.randint(jax.random.fold_in(own_key, 1), (couples,), 0, 1 << 20) % (room + 1)
    sizes = sizes.at[1:1 + 2 * couples:2].set(source_of - shifted).at[2:2 + 2 * couples:2].set(sink + shifted)
    return sizes[jax.random.permutation(jax.random.fold_in(own_key, 2), number_of)]


def normal_values(rng, shape, scale, reach, split=(), kind=jnp.bfloat16):
    factor_of = shard_levels(rng, shape, split, -0.22, 0.18) if split else 1.0
    values = jax.random.normal(rng, shape, jnp.float32) * scale * factor_of
    return jnp.minimum(jnp.maximum(values, -reach), reach).astype(kind)


def setup_inputs(seed: int = 0) -> dict:
    key_list = jax.random.split(jax.random.key(seed), 8)
    return {
        "state": normal_values(key_list[0], (M, TILES, TILE_CELLS), 1.0, 6.0, ((1, 8), (2, 16)), jnp.float32),
        "obs_rows": normal_values(key_list[1], (BATCHES, M, TILES, K_DEV), 1.0, 6.0, ((0, 16), (2, 8)), jnp.float32),
        "obs_value": normal_values(key_list[2], (BATCHES, TILES, K_DEV), 1.5, 6.0, ((0, 16), (1, 8)), jnp.float32),
        "obs_noise": jnp.clip(jnp.exp(math.log(3.0) - 2.3025851 * jax.random.uniform(key_list[3], (BATCHES, TILES, K_DEV), jnp.float32) ** shard_levels(key_list[3], (BATCHES, TILES, K_DEV), ((0, 16), (1, 8)), -0.2, 0.2)), 0.3, 3.0),
        "obs_cell": place_ends(jax.random.randint(key_list[4], (BATCHES, TILES, K_DEV), 0, TILE_CELLS), jax.random.fold_in(key_list[4], 1), 0, TILE_CELLS - 1).astype(jnp.int32),
        "obs_class": place_ends(jax.random.randint(key_list[5], (BATCHES, TILES, K_DEV), 0, 3), jax.random.fold_in(key_list[5], 1), 0, 2).astype(jnp.int32),
        "obs_count": jax.vmap(lambda own: uneven(own, TILES, TILES * K_DEV // 2, K_DEV, 2))(jax.random.split(key_list[6], BATCHES)).reshape((BATCHES, TILES)).astype(jnp.int32),
    }


PRECISE = lax.Precision.HIGHEST
EPSILON = 1e-06
DIMS_CROSS = (((0,), (0,)), ((), ()))
DIMS_APPLY = (((1,), (1,)), ((), ()))

def taper(distance, inv_width):
    nearness = jnp.maximum(1.0 - distance * inv_width, 0.0)
    return nearness * nearness

def batch_terms(rows_now, obs_val, noise_var, live_mask):
    members = rows_now.shape[0]
    ens_mean = lax.optimization_barrier(jnp.mean(rows_now, axis=0))
    anomaly = rows_now - ens_mean[None]
    prior_var = lax.optimization_barrier(jnp.sum(anomaly * anomaly, axis=0)) / (members - 1) + EPSILON
    post_var = 1.0 / (1.0 / prior_var + 1.0 / noise_var)
    post_mean = post_var * (ens_mean / prior_var + obs_val / noise_var)
    shift_term = jnp.where(live_mask, post_mean - ens_mean, 0.0)
    factor = jnp.where(live_mask, jnp.sqrt(post_var / prior_var) - 1.0, 0.0)
    obs_scale = 1.0 / ((members - 1) * prior_var)
    return (anomaly, shift_term, factor, obs_scale)

def regress(target, target_pos, anomaly, increment, obs_scale, source_pos, inv_width):
    centered = target - lax.optimization_barrier(jnp.mean(target, axis=0))[None]
    covariance = lax.dot_general(centered, anomaly, DIMS_CROSS, precision=PRECISE, preferred_element_type=jnp.float32)
    weights = taper(jnp.abs(target_pos[:, None] - source_pos[None, :]), inv_width[None, :])
    gain = weights * (covariance * obs_scale[None, :])
    return target + lax.dot_general(increment, gain, DIMS_APPLY, precision=PRECISE, preferred_element_type=jnp.float32)

def pad_tiles(values):
    spec = [(0, 0)] * (values.ndim - 2) + [(1, 1), (0, 0)]
    return jnp.pad(values, spec)

def reference(state, obs_rows, obs_value, obs_noise, obs_cell, obs_class, obs_count):
    members, tiles, tile_width = state.shape
    nbatch = obs_rows.shape[0]
    slot_count = obs_rows.shape[3]
    tile_start = jnp.arange(tiles, dtype=jnp.int32) * tile_width
    cell_pos = (tile_start[:, None] + jnp.arange(tile_width, dtype=jnp.int32)[None, :]).astype(jnp.float32)
    obs_pos = (tile_start[None, :, None] + obs_cell).astype(jnp.float32)
    inv_width = 4.0 / (tile_width * (obs_class + 2).astype(jnp.float32))
    live_all = jnp.arange(slot_count, dtype=jnp.int32)[None, None, :] < obs_count[:, :, None]
    current = obs_rows
    for batch_step in range(nbatch):
        anomaly, shift_term, factor, obs_scale = batch_terms(current[batch_step], obs_value[batch_step], obs_noise[batch_step], live_all[batch_step])
        increment = shift_term[None] + factor[None] * anomaly
        anomaly_pad = pad_tiles(anomaly)
        increment_pad = pad_tiles(increment)
        scale_pad = pad_tiles(obs_scale)
        pos_pad = pad_tiles(obs_pos[batch_step])
        inv_pad = pad_tiles(inv_width[batch_step])
        state_now = state
        rows_now = current

        def one_tile(tile_index):

            def pick_tiles(values):
                return lax.dynamic_slice_in_dim(values, tile_index, 3, values.ndim - 2)
            src_anomaly = pick_tiles(anomaly_pad).reshape(members, 3 * slot_count)
            src_increment = pick_tiles(increment_pad).reshape(members, 3 * slot_count)
            src_scale = pick_tiles(scale_pad).reshape(3 * slot_count)
            src_pos = pick_tiles(pos_pad).reshape(3 * slot_count)
            src_inv = pick_tiles(inv_pad).reshape(3 * slot_count)
            tile_cells = lax.dynamic_index_in_dim(state_now, tile_index, 1, False)
            tile_rows = lax.dynamic_index_in_dim(rows_now, tile_index, 2, False)
            tile_rows = jnp.transpose(tile_rows, (1, 0, 2)).reshape(members, nbatch * slot_count)
            target = jnp.concatenate([tile_cells, tile_rows], axis=1)
            row_pos = lax.dynamic_index_in_dim(obs_pos, tile_index, 1, False).reshape(nbatch * slot_count)
            target_pos = jnp.concatenate([lax.dynamic_index_in_dim(cell_pos, tile_index, 0, False), row_pos])
            return regress(target, target_pos, src_anomaly, src_increment, src_scale, src_pos, src_inv)
        result = lax.map(one_tile, jnp.arange(tiles, dtype=jnp.int32))
        state = jnp.transpose(result[:, :, :tile_width], (1, 0, 2))
        new_rows = result[:, :, tile_width:].reshape(tiles, members, nbatch, slot_count)
        new_rows = jnp.transpose(new_rows, (2, 1, 0, 3))
        later_mask = (jnp.arange(nbatch, dtype=jnp.int32) > batch_step)[:, None, None, None]
        current = jnp.where(later_mask, new_rows, current)
    return state
```

```python
import jax
import jax.numpy as jnp
from jax import lax
from jax.experimental import pallas as pl
from jax.experimental.pallas import tpu as pltpu
from jax.sharding import PartitionSpec as P

EPSILON = 1e-06
META = 8
WIDE = 256
ROOM = 32 * 1024 * 1024
F32 = jnp.float32
BF16 = jnp.bfloat16


def split(x):
    hi = x.astype(BF16).astype(F32)
    return hi, x - hi


def terms(block, members):
    rows = block[:members]
    meta = block[members : members + META]
    val, noise, pos, half, live = (meta[i : i + 1] for i in range(5))
    mean = jnp.sum(rows, axis=0, keepdims=True) / members
    an = rows - mean
    var = jnp.sum(an * an, axis=0, keepdims=True) / (members - 1) + EPSILON
    post_var = 1.0 / (1.0 / var + 1.0 / noise)
    post_mean = post_var * (mean / var + val / noise)
    shift = jnp.where(live > 0.5, post_mean - mean, 0.0)
    factor = jnp.where(live > 0.5, jnp.sqrt(post_var / var) - 1.0, 0.0)
    scale = 1.0 / ((members - 1) * var * (half * half))
    slots = rows.shape[1]
    a_hi, a_lo = split(an * scale)
    stack = jnp.concatenate(
        [a_hi, a_hi, a_lo, pos, half, jnp.zeros((WIDE - 3 * members - 2, slots), F32)], axis=0
    )
    turned = jnp.transpose(stack)
    at = turned.astype(BF16)
    pb = jnp.broadcast_to(turned[:, 3 * members : 3 * members + 1], (slots, slots))
    hb = jnp.broadcast_to(turned[:, 3 * members + 1 : 3 * members + 2], (slots, slots))
    inc = shift + factor * an
    i_hi, i_lo = split(inc)
    lower = jnp.concatenate([i_lo, jnp.zeros_like(i_lo)], axis=1)
    left = jnp.concatenate([jnp.concatenate([i_hi, i_hi], axis=1), lower], axis=0).astype(BF16)
    return at, left, pb, hb


def apply(z, tpos, at, left, pbs, hbs):
    members, n = z.shape
    zc = z - jnp.sum(z, axis=0, keepdims=True) / members
    z_hi, z_lo = split(zc)
    zst = jnp.concatenate(
        [z_hi, z_lo, z_hi, jnp.zeros((WIDE - 3 * members, n), F32)], axis=0
    ).astype(BF16)
    cov = jnp.dot(at, zst, preferred_element_type=F32)
    gains = []
    slots = pbs[0].shape[0]
    for j in range(len(pbs)):
        reps = n // pbs[j].shape[1]
        pb = jnp.concatenate([pbs[j]] * reps, axis=1) if reps > 1 else pbs[j]
        hb = jnp.concatenate([hbs[j]] * reps, axis=1) if reps > 1 else hbs[j]
        m = jnp.maximum(hb - jnp.abs(tpos - pb), 0.0)
        g = m * (m * cov[j * slots : (j + 1) * slots])
        g_hi = g.astype(BF16)
        g_lo = (g - g_hi.astype(F32)).astype(BF16)
        gains += [g_hi, g_lo]
    acc = jnp.dot(left, jnp.concatenate(gains, axis=0), preferred_element_type=F32)
    return z + acc[:members] + acc[members:]


def window(refs, step, t, slots):
    at_ref, left_ref, pb_ref, hb_ref = refs
    return (
        at_ref[step, t * slots : (t + 3) * slots],
        left_ref[step, :, t * 2 * slots : (t + 3) * 2 * slots],
        [pb_ref[step, t + j] for j in range(3)],
        [hb_ref[step, t + j] for j in range(3)],
    )


def vmem(shape, dtype):
    return pltpu.VMEM(shape, dtype)


def inside(*arrays):
    return [pltpu.with_memory_space_constraint(a, pltpu.VMEM) for a in arrays]


def make_crit(members, slots, pair):
    full = members + META
    last = pair is None

    def crit(x_ref, y_ref, o_ref, e_ref, *rest):
        if last:
            refs = rest
        else:
            r_ref, *refs, xn_ref, yn_ref, zs_ref = rest

        def keep(step, j, pack):
            at, left, pb, hb = pack
            refs[0][step, j * slots : (j + 1) * slots] = at
            refs[1][step, :, j * 2 * slots : (j + 1) * 2 * slots] = left
            refs[2][step, j] = pb
            refs[3][step, j] = hb

        first = [o_ref[1], o_ref[0], x_ref[0], x_ref[1], e_ref[0], e_ref[1]]
        packs = [terms(b, members) for b in first]
        for j in range(4):
            keep(0, j, packs[j + 1])
        second = [o_ref[2], x_ref[2], y_ref[...], e_ref[2]]
        for j in range(4):
            near = packs[j : j + 3]
            block = second[j]
            new = apply(
                block[:members],
                block[members + 2 : members + 3],
                jnp.concatenate([q[0] for q in near], axis=0),
                jnp.concatenate([q[1] for q in near], axis=1),
                [q[2] for q in near],
                [q[3] for q in near],
            )
            keep(1, j, terms(jnp.concatenate([new, block[members:]], axis=0), members))
        if not last:
            wide = []
            for t in range(2):
                wide.append(jnp.concatenate([r_ref[pair, t, 0], r_ref[pair, t, 1]], axis=1))
                zs_ref[t] = wide[t][:members]

            def one(step, carry):
                new = [
                    apply(
                        zs_ref[t],
                        wide[t][members + 2 : members + 3],
                        *window(refs, step, t, slots),
                    )
                    for t in range(2)
                ]
                for t in range(2):
                    zs_ref[t] = new[t]
                return carry

            lax.fori_loop(0, 2, one, 0)
            for t in range(2):
                done = jnp.concatenate([zs_ref[t], wide[t][members:]], axis=0)
                xn_ref[t] = done[:, :slots]
                if t == 0:
                    xn_ref[2] = done[:, slots:]
                else:
                    yn_ref[...] = done[:, slots:]

    pack_shapes = (
        vmem((2, 4 * slots, WIDE), BF16),
        vmem((2, 2 * members, 8 * slots), BF16),
        vmem((2, 4, slots, slots), F32),
        vmem((2, 4, slots, slots), F32),
    )
    next_shapes = (vmem((3, full, slots), F32), vmem((full, slots), F32))
    return pl.pallas_call(
        crit,
        out_shape=pack_shapes if last else pack_shapes + next_shapes,
        scratch_shapes=() if last else (pltpu.VMEM((2, members, 2 * slots), F32),),
        compiler_params=pltpu.CompilerParams(vmem_limit_bytes=ROOM),
        name="crit",
    )


def make_trail(members, slots, begin, groups, cells):
    part = min(cells // 2, 2 * slots)
    rows_too = begin < groups - 1

    def trail(*all_refs):
        if rows_too:
            *refs, cpos_ref, s_ref, r_ref, so_ref, ro_ref, zs_ref = all_refs
        else:
            *refs, cpos_ref, s_ref, so_ref, zs_ref = all_refs

        def both_steps(tpos, sides):
            def one(step, carry):
                new = [
                    apply(zs_ref[i], tpos[i], *window(refs, step, sides[i], slots))
                    for i in range(2)
                ]
                for i in range(2):
                    zs_ref[i] = new[i]
                return carry

            lax.fori_loop(0, 2, one, 0)

        if rows_too:

            def rows_step(p, carry):
                tpos = []
                for t in range(2):
                    both = jnp.concatenate([r_ref[p, t, 0], r_ref[p, t, 1]], axis=1)
                    zs_ref[t] = both[:members]
                    tpos.append(both[members + 2 : members + 3])
                    for k in range(2):
                        ro_ref[p, t, k, members:] = r_ref[p, t, k, members:]
                both_steps(tpos, (0, 1))
                for t in range(2):
                    ro_ref[p, t, 0, :members] = zs_ref[t, :, :slots]
                    ro_ref[p, t, 1, :members] = zs_ref[t, :, slots:]
                return carry

            lax.fori_loop(begin, groups - 1, rows_step, 0)

        def cells_step(c, carry):
            ats = [
                pl.ds(pl.multiple_of((2 * c + i) * part, part), part) for i in range(2)
            ]
            for i in range(2):
                zs_ref[i] = s_ref[:, ats[i]]
            both_steps([cpos_ref[:, ats[i]] for i in range(2)], (0, 0))
            for i in range(2):
                so_ref[:, ats[i]] = zs_ref[i]
            return carry

        lax.fori_loop(0, cells // (2 * part), cells_step, 0)

    shapes = (vmem((members, cells), F32),)
    if rows_too:
        shapes += (vmem((groups - 1, 2, 2, members + META, slots), F32),)
    return pl.pallas_call(
        trail,
        out_shape=shapes,
        input_output_aliases={5: 0, 6: 1} if rows_too else {5: 0},
        scratch_shapes=(pltpu.VMEM((2, members, part), F32),),
        compiler_params=pltpu.CompilerParams(vmem_limit_bytes=ROOM),
        name="trail",
    )


def on_device(state, obs_rows, obs_value, obs_noise, obs_cell, obs_class, obs_count):
    members, _, cells = state.shape
    slots = obs_rows.shape[3]
    nbatch = lax.axis_size("region")
    tiles = lax.axis_size("tile")
    chips = tiles // 2
    region_index = lax.axis_index("region")
    tile_index = lax.axis_index("tile")
    tile_width = cells * nbatch
    cell_pos = (
        tile_index * tile_width + region_index * cells + jnp.arange(cells, dtype=jnp.int32)
    ).astype(F32)[None]
    pos = (tile_index * tile_width + obs_cell[0, 0]).astype(F32)
    half = (tile_width / 4) * (obs_class[0, 0] + 2).astype(F32)
    live = (jnp.arange(slots, dtype=jnp.int32) < obs_count[0, 0]).astype(F32)
    zero = jnp.zeros_like(pos)
    block = jnp.concatenate(
        [
            obs_rows[0, :, 0, :],
            jnp.stack([obs_value[0, 0], obs_noise[0, 0], pos, half, live, zero, zero, zero]),
        ],
        axis=0,
    )
    own = lax.all_to_all(
        jnp.broadcast_to(block[None], (nbatch,) + block.shape), "region", 0, 0, tiled=True
    )
    other = lax.ppermute(own, "tile", [(i, i ^ 1) for i in range(tiles)])
    swap = []
    slide = []
    for z in range(chips):
        up = (z + 1) % chips
        down = (z - 1) % chips
        swap += [(2 * z + 1, 2 * up), (2 * z, 2 * down + 1)]
        slide += [(2 * z + 1, 2 * up + 1), (2 * z, 2 * down)]
    groups = nbatch // 2
    x = jnp.stack([own[0], other[0], own[1]])
    y = other[1]
    rest = jnp.stack([own[2:], other[2:]])
    rest = rest.reshape(2, groups - 1, 2, *block.shape).transpose(1, 0, 2, 3, 4)
    cells_now = state[:, 0, :]
    for g in range(groups):
        o = lax.ppermute(x, "tile", swap)
        e = lax.ppermute(x, "tile", slide)
        last = g == groups - 1
        crit = make_crit(members, slots, None if last else g)
        if last:
            packs = crit(*inside(x, y, o, e))
        else:
            *packs, x, y = crit(*inside(x, y, o, e, rest))
        trail = make_trail(members, slots, g + 1, groups, cells)
        if g + 1 < groups - 1:
            cells_now, rest = trail(*inside(*packs, cell_pos, cells_now, rest))
        else:
            (cells_now,) = trail(*inside(*packs, cell_pos, cells_now))
    return cells_now[:, None, :]


def solution(mesh):
    placed = (
        P(None, "tile", "region"),
        P("region", None, "tile", None),
        P("region", "tile", None),
        P("region", "tile", None),
        P("region", "tile", None),
        P("region", "tile", None),
        P("region", "tile"),
    )
    return jax.shard_map(
        on_device, mesh=mesh, in_specs=placed, out_specs=P(None, "tile", "region"), check_vma=False
    )
```

```python
import jax
import jax.numpy as jnp
from jax import lax
from jax.experimental import pallas as pl
from jax.experimental.pallas import tpu as pltpu
from jax.sharding import PartitionSpec as P

EPSILON = 1e-06
META = 8
WIDE = 256
ROOM = 32 * 1024 * 1024
F32 = jnp.float32
BF16 = jnp.bfloat16


def split(x):
    hi = x.astype(BF16).astype(F32)
    return hi, x - hi


def terms(block, members):
    rows = block[:members]
    meta = block[members : members + META]
    val, noise, pos, half, live = (meta[i : i + 1] for i in range(5))
    mean = jnp.sum(rows, axis=0, keepdims=True) / members
    an = rows - mean
    var = jnp.sum(an * an, axis=0, keepdims=True) / (members - 1) + EPSILON
    post_var = 1.0 / (1.0 / var + 1.0 / noise)
    post_mean = post_var * (mean / var + val / noise)
    shift = jnp.where(live > 0.5, post_mean - mean, 0.0)
    factor = jnp.where(live > 0.5, jnp.sqrt(post_var / var) - 1.0, 0.0)
    scale = 1.0 / ((members - 1) * var * (half * half))
    slots = rows.shape[1]
    a_hi, a_lo = split(an * scale)
    p_hi, p_rest = split(pos)
    p_mid, p_lo = split(p_rest)
    stack = jnp.concatenate(
        [
            *(a_hi, a_hi, a_lo, half, p_hi, p_mid, p_lo, pos),
            jnp.zeros((WIDE - 3 * members - 5, slots), F32),
        ],
        axis=0,
    )
    turned = jnp.transpose(stack)
    at = turned.astype(BF16)
    pb = jnp.broadcast_to(turned[:, 3 * members + 4 : 3 * members + 5], (slots, slots))
    hb = jnp.broadcast_to(turned[:, 3 * members : 3 * members + 1], (slots, slots))
    inc = shift + factor * an
    i_hi, i_lo = split(inc)
    lower = jnp.concatenate([i_lo, jnp.zeros_like(i_lo)], axis=1)
    left = jnp.concatenate([jnp.concatenate([i_hi, i_hi], axis=1), lower], axis=0).astype(BF16)
    return at, left, pb, hb


def centered(z):
    members, n = z.shape
    zc = z - jnp.sum(z, axis=0, keepdims=True) / members
    z_hi, z_lo = split(zc)
    return jnp.concatenate(
        [z_hi, z_lo, z_hi, jnp.zeros((WIDE - 3 * members, n), F32)], axis=0
    ).astype(BF16)


def change(zst, tpos, at, left, pbs, hbs):
    n = zst.shape[1]
    cov = jnp.dot(at, zst, preferred_element_type=F32)
    gains = []
    slots = pbs[0].shape[0]
    for j in range(len(pbs)):
        reps = n // pbs[j].shape[1]
        pb = jnp.concatenate([pbs[j]] * reps, axis=1) if reps > 1 else pbs[j]
        hb = jnp.concatenate([hbs[j]] * reps, axis=1) if reps > 1 else hbs[j]
        m = jnp.maximum(hb - jnp.abs(tpos - pb), 0.0)
        g = m * (m * cov[j * slots : (j + 1) * slots])
        g_hi = g.astype(BF16)
        g_lo = (g - g_hi.astype(F32)).astype(BF16)
        gains += [g_hi, g_lo]
    acc = jnp.dot(left, jnp.concatenate(gains, axis=0), preferred_element_type=F32)
    members = left.shape[0] // 2
    return acc[:members] + acc[members:]


def apply(z, tpos, *sources):
    return z + change(centered(z), tpos, *sources)


def window(refs, step, t, slots):
    at_ref, left_ref, pb_ref, hb_ref, _ = refs
    return (
        at_ref[step, t * slots : (t + 3) * slots],
        left_ref[step, :, t * 2 * slots : (t + 3) * 2 * slots],
        [pb_ref[step, t + j] for j in range(3)],
        [hb_ref[step, t + j] for j in range(3)],
    )


def vmem(shape, dtype):
    return pltpu.VMEM(shape, dtype)


def inside(*arrays):
    return [pltpu.with_memory_space_constraint(a, pltpu.VMEM) for a in arrays]


def make_crit(members, slots, last):
    full = members + META

    def crit(x_ref, y_ref, o_ref, e_ref, *rest):
        if last:
            refs = rest
        else:
            *r_refs, a, b, c, d, m, xn_ref, yn_ref, zs_ref = rest
            refs = (a, b, c, d, m)

        def keep(step, j, pack, meta):
            at, left, pb, hb = pack
            refs[0][step, j * slots : (j + 1) * slots] = at
            refs[1][step, :, j * 2 * slots : (j + 1) * 2 * slots] = left
            refs[2][step, j] = pb
            refs[3][step, j] = hb
            refs[4][step, :, j * slots : (j + 1) * slots] = meta

        first = [o_ref[1], o_ref[0], x_ref[0], x_ref[1], e_ref[0], e_ref[1]]
        packs = [terms(b, members) for b in first]
        for j in range(4):
            keep(0, j, packs[j + 1], first[j + 1][members:])
        second = [o_ref[2], x_ref[2], y_ref[...], e_ref[2]]
        for j in range(4):
            near = packs[j : j + 3]
            block = second[j]
            new = apply(
                block[:members],
                block[members + 2 : members + 3],
                jnp.concatenate([q[0] for q in near], axis=0),
                jnp.concatenate([q[1] for q in near], axis=1),
                [q[2] for q in near],
                [q[3] for q in near],
            )
            new = jnp.concatenate([new, block[members:]], axis=0)
            keep(1, j, terms(new, members), block[members:])
        if not last:
            wide = []
            for t in range(2):
                wide.append(jnp.concatenate([r_refs[t][0], r_refs[t][1]], axis=1))
                zs_ref[t] = wide[t][:members]

            def one(step, carry):
                new = [
                    apply(
                        zs_ref[t],
                        wide[t][members + 2 : members + 3],
                        *window(refs, step, t, slots),
                    )
                    for t in range(2)
                ]
                for t in range(2):
                    zs_ref[t] = new[t]
                return carry

            lax.fori_loop(0, 2, one, 0)
            for t in range(2):
                done = jnp.concatenate([zs_ref[t], wide[t][members:]], axis=0)
                xn_ref[t] = done[:, :slots]
                if t == 0:
                    xn_ref[2] = done[:, slots:]
                else:
                    yn_ref[...] = done[:, slots:]

    pack_shapes = (
        vmem((2, 4 * slots, WIDE), BF16),
        vmem((2, 2 * members, 8 * slots), BF16),
        vmem((2, 4, slots, slots), F32),
        vmem((2, 4, slots, slots), F32),
        vmem((2, META, 4 * slots), F32),
    )
    next_shapes = (vmem((3, full, slots), F32), vmem((full, slots), F32))
    return pl.pallas_call(
        crit,
        out_shape=pack_shapes if last else pack_shapes + next_shapes,
        scratch_shapes=() if last else (pltpu.VMEM((2, members, 2 * slots), F32),),
        compiler_params=pltpu.CompilerParams(vmem_limit_bytes=ROOM),
        name="crit",
    )


def run_steps(zs_ref, tpos, refs, t, slots):
    def one(step, carry):
        new = [
            apply(zs_ref[i], tpos[i], *window(refs, step, t, slots)) for i in range(len(tpos))
        ]
        for i in range(len(tpos)):
            zs_ref[i] = new[i]
        return carry

    lax.fori_loop(0, 2, one, 0)


def make_rows(members, slots, begin, groups):
    full = members + META

    def rows(*all_refs):
        *refs, r_ref, n_ref, ro_ref, zs_ref = all_refs
        for p in range(begin, groups, 2):
            some = range(p, min(p + 2, groups))
            tpos = []
            for i, q in enumerate(some):
                both = jnp.concatenate([r_ref[q, 0], r_ref[q, 1]], axis=1)
                zs_ref[i] = both[:members]
                tpos.append(both[members + 2 : members + 3])
            run_steps(zs_ref, tpos, refs, 0, slots)
            for i, q in enumerate(some):
                for k in range(2):
                    if q == begin:
                        n_ref[k, :members] = zs_ref[i, :, k * slots : (k + 1) * slots]
                        n_ref[k, members:] = r_ref[q, k, members:]
                    else:
                        ro_ref[q, k, :members] = zs_ref[i, :, k * slots : (k + 1) * slots]
                        ro_ref[q, k, members:] = r_ref[q, k, members:]

    return pl.pallas_call(
        rows,
        out_shape=(vmem((2, full, slots), F32), vmem((groups, 2, full, slots), F32)),
        input_output_aliases={5: 1},
        scratch_shapes=(pltpu.VMEM((2, members, 2 * slots), F32),),
        compiler_params=pltpu.CompilerParams(vmem_limit_bytes=ROOM),
        name="rows",
    )


def make_cells(members, slots, cells, step):
    part = min(cells, 2 * slots)
    chains = min(4, cells // part)
    span = 3 * slots

    def update(*all_refs):
        at_ref, left_ref, meta_ref, tri_ref, cpos_ref, s_ref, so_ref, *work = all_refs
        atc_ref, leftc_ref, pbc_ref, hbc_ref, zst_ref = work
        meta = meta_ref[step, :, :span]
        pos, half, live = meta[2:3], meta[3:4], meta[4:5]
        begin, end = cpos_ref[:, :1], cpos_ref[:, cells - 1 :]
        near = jnp.where((pos + half > begin) & (pos - half < end), live, 0.0)
        before = jnp.dot(
            jnp.broadcast_to(near, (16, span)).astype(BF16),
            tri_ref[...],
            preferred_element_type=F32,
        )
        spot = jnp.where(near > 0.5, before[:1], -1.0)
        count = (jnp.sum(near).astype(jnp.int32) + (slots - 1)) // slots
        lefts = jnp.concatenate(
            [left_ref[step, :, 2 * t * slots : (2 * t + 1) * slots] for t in range(3)], axis=1
        )

        def pick(c):
            rank = lax.broadcasted_iota(jnp.int32, (slots, span), 0) + c * slots
            hot = jnp.where(rank.astype(F32) == spot, 1.0, 0.0).astype(BF16)
            got = jnp.dot(hot, at_ref[step, :span], preferred_element_type=F32)
            atc_ref[c] = got.astype(BF16)
            k = 3 * members
            where = got[:, k + 1 : k + 2] + got[:, k + 2 : k + 3] + got[:, k + 3 : k + 4]
            pbc_ref[c] = jnp.broadcast_to(where, (slots, slots))
            hbc_ref[c] = jnp.broadcast_to(got[:, k : k + 1], (slots, slots))
            inc = lax.dot_general(
                lefts, hot, (((1,), (1,)), ((), ())), preferred_element_type=F32
            )
            high, low = inc[:members], inc[members:]
            leftc_ref[c] = jnp.concatenate(
                [
                    jnp.concatenate([high, high], axis=1),
                    jnp.concatenate([low, jnp.zeros_like(low)], axis=1),
                ],
                axis=0,
            ).astype(BF16)

        def looped(body):
            def one(c, carry):
                body(c)
                return carry

            lax.fori_loop(1, count, one, 0)

        pick(0)
        looped(pick)

        def add(c, ats):
            for i, a in enumerate(ats):
                so_ref[:, a] = so_ref[:, a] + change(
                    zst_ref[i], cpos_ref[:, a], atc_ref[c], leftc_ref[c], [pbc_ref[c]], [hbc_ref[c]]
                )

        def cells_step(n, carry):
            ats = [
                pl.ds(pl.multiple_of((chains * n + i) * part, part), part) for i in range(chains)
            ]
            new = []
            for i, a in enumerate(ats):
                z = s_ref[:, a]
                zst = centered(z)
                zst_ref[i] = zst
                new.append(
                    z
                    + change(
                        zst, cpos_ref[:, a], atc_ref[0], leftc_ref[0], [pbc_ref[0]], [hbc_ref[0]]
                    )
                )
            for i, a in enumerate(ats):
                so_ref[:, a] = new[i]
            looped(lambda c: add(c, ats))
            return carry

        lax.fori_loop(0, cells // (chains * part), cells_step, 0)

    return pl.pallas_call(
        update,
        out_shape=vmem((members, cells), F32),
        input_output_aliases={5: 0},
        scratch_shapes=(
            pltpu.VMEM((3, slots, WIDE), BF16),
            pltpu.VMEM((3, 2 * members, 2 * slots), BF16),
            pltpu.VMEM((3, slots, slots), F32),
            pltpu.VMEM((3, slots, slots), F32),
            pltpu.VMEM((chains, WIDE, part), BF16),
        ),
        compiler_params=pltpu.CompilerParams(vmem_limit_bytes=ROOM),
        name="cells",
    )


def on_device(state, obs_rows, obs_value, obs_noise, obs_cell, obs_class, obs_count):
    members, _, cells = state.shape
    slots = obs_rows.shape[3]
    nbatch = lax.axis_size("region")
    tiles = lax.axis_size("tile")
    chips = tiles // 2
    region_index = lax.axis_index("region")
    tile_index = lax.axis_index("tile")
    tile_width = cells * nbatch
    cell_pos = (
        tile_index * tile_width + region_index * cells + jnp.arange(cells, dtype=jnp.int32)
    ).astype(F32)[None]
    pos = (tile_index * tile_width + obs_cell[0, 0]).astype(F32)
    half = (tile_width / 4) * (obs_class[0, 0] + 2).astype(F32)
    live = (jnp.arange(slots, dtype=jnp.int32) < obs_count[0, 0]).astype(F32)
    zero = jnp.zeros_like(pos)
    block = jnp.concatenate(
        [
            obs_rows[0, :, 0, :],
            jnp.stack([obs_value[0, 0], obs_noise[0, 0], pos, half, live, zero, zero, zero]),
        ],
        axis=0,
    )
    own = lax.all_to_all(
        jnp.broadcast_to(block[None], (nbatch,) + block.shape), "region", 0, 0, tiled=True
    )
    partner = [(i, i ^ 1) for i in range(tiles)]
    across = []
    for z in range(chips):
        across += [(2 * z + 1, 2 * ((z + 1) % chips)), (2 * z, 2 * ((z - 1) % chips) + 1)]
    groups = nbatch // 2
    begun = min(nbatch, 4)
    other = lax.ppermute(own[:begun], "tile", partner)
    x = jnp.stack([own[0], other[0], own[1]])
    y = other[1]
    near = own[2:4]
    far = other[2:4]
    rest = own.reshape(groups, 2, *block.shape)
    cells_now = state[:, 0, :]
    order = jnp.arange(3 * slots, dtype=jnp.int32)
    tri = (order[:, None] < order[None, :]).astype(BF16)

    def update(step, packs, cells_now):
        at, left, _, _, meta = packs
        kernel = make_cells(members, slots, cells, step)
        return kernel(*inside(at, left, meta, tri, cell_pos, cells_now))

    for g in range(groups):
        o = lax.ppermute(x, "tile", across)
        if g > 0:
            cells_now = update(0, packs, cells_now)
            o, cells_now = lax.optimization_barrier((o, cells_now))
        if g > 0 and g + 1 < groups:
            near, rest = make_rows(members, slots, g + 1, groups)(*inside(*packs, rest))
            o, near = lax.optimization_barrier((o, near))
            far = lax.ppermute(near, "tile", partner)
        e = lax.ppermute(o, "tile", partner)
        if g > 0:
            cells_now = update(1, packs, cells_now)
            e, far, cells_now = lax.optimization_barrier((e, far, cells_now))
        last = g == groups - 1
        crit = make_crit(members, slots, last)
        if last:
            packs = crit(*inside(x, y, o, e))
        else:
            *packs, x, y = crit(*inside(x, y, o, e, near, far))
    for step in range(2):
        cells_now = update(step, packs, cells_now)
    return cells_now[:, None, :]


def solution(mesh):
    placed = (
        P(None, "tile", "region"),
        P("region", None, "tile", None),
        P("region", "tile", None),
        P("region", "tile", None),
        P("region", "tile", None),
        P("region", "tile", None),
        P("region", "tile"),
    )
    return jax.shard_map(
        on_device, mesh=mesh, in_specs=placed, out_specs=P(None, "tile", "region"), check_vma=False
    )
```

```python
import jax
import jax.numpy as jnp
from jax import lax
from jax.experimental import pallas as pl
from jax.experimental.pallas import tpu as pltpu
from jax.sharding import PartitionSpec as P

EPSILON = 1e-06
META = 8
WIDE = 256
ROOM = 32 * 1024 * 1024
F32 = jnp.float32
BF16 = jnp.bfloat16


def split(x):
    hi = x.astype(BF16).astype(F32)
    return hi, x - hi


def terms(block, members):
    rows = block[:members]
    meta = block[members : members + META]
    val, noise, pos, half, live = (meta[i : i + 1] for i in range(5))
    mean = jnp.sum(rows, axis=0, keepdims=True) / members
    an = rows - mean
    var = jnp.sum(an * an, axis=0, keepdims=True) / (members - 1) + EPSILON
    post_var = 1.0 / (1.0 / var + 1.0 / noise)
    post_mean = post_var * (mean / var + val / noise)
    shift = jnp.where(live > 0.5, post_mean - mean, 0.0)
    factor = jnp.where(live > 0.5, jnp.sqrt(post_var / var) - 1.0, 0.0)
    scale = 1.0 / ((members - 1) * var * (half * half))
    slots = rows.shape[1]
    a_hi, a_lo = split(an * scale)
    p_hi, p_rest = split(pos)
    p_mid, p_lo = split(p_rest)
    stack = jnp.concatenate(
        [
            *(a_hi, a_hi, a_lo, half, p_hi, p_mid, p_lo, pos),
            jnp.zeros((WIDE - 3 * members - 5, slots), F32),
        ],
        axis=0,
    )
    turned = jnp.transpose(stack)
    at = turned.astype(BF16)
    pb = jnp.broadcast_to(turned[:, 3 * members + 4 : 3 * members + 5], (slots, slots))
    hb = jnp.broadcast_to(turned[:, 3 * members : 3 * members + 1], (slots, slots))
    inc = shift + factor * an
    i_hi, i_lo = split(inc)
    lower = jnp.concatenate([i_lo, jnp.zeros_like(i_lo)], axis=1)
    left = jnp.concatenate([jnp.concatenate([i_hi, i_hi], axis=1), lower], axis=0).astype(BF16)
    return at, left, pb, hb


def centered(z):
    members, n = z.shape
    zc = z - jnp.sum(z, axis=0, keepdims=True) / members
    z_hi, z_lo = split(zc)
    return jnp.concatenate(
        [z_hi, z_lo, z_hi, jnp.zeros((WIDE - 3 * members, n), F32)], axis=0
    ).astype(BF16)


def change(zst, tpos, at, left, pbs, hbs):
    n = zst.shape[1]
    cov = jnp.dot(at, zst, preferred_element_type=F32)
    gains = []
    slots = pbs[0].shape[0]
    for j in range(len(pbs)):
        reps = n // pbs[j].shape[1]
        pb = jnp.concatenate([pbs[j]] * reps, axis=1) if reps > 1 else pbs[j]
        hb = jnp.concatenate([hbs[j]] * reps, axis=1) if reps > 1 else hbs[j]
        m = jnp.maximum(hb - jnp.abs(tpos - pb), 0.0)
        g = m * (m * cov[j * slots : (j + 1) * slots])
        g_hi = g.astype(BF16)
        g_lo = (g - g_hi.astype(F32)).astype(BF16)
        gains += [g_hi, g_lo]
    acc = jnp.dot(left, jnp.concatenate(gains, axis=0), preferred_element_type=F32)
    members = left.shape[0] // 2
    return acc[:members] + acc[members:]


def apply(z, tpos, *sources):
    return z + change(centered(z), tpos, *sources)


def window(refs, step, t, slots):
    at_ref, left_ref, pb_ref, hb_ref, _ = refs
    return (
        at_ref[step, t * slots : (t + 3) * slots],
        left_ref[step, :, t * 2 * slots : (t + 3) * 2 * slots],
        [pb_ref[step, t + j] for j in range(3)],
        [hb_ref[step, t + j] for j in range(3)],
    )


def vmem(shape, dtype):
    return pltpu.VMEM(shape, dtype)


def inside(*arrays):
    return [pltpu.with_memory_space_constraint(a, pltpu.VMEM) for a in arrays]


def make_crit(members, slots, last):
    full = members + META

    def crit(x_ref, y_ref, o_ref, e_ref, *rest):
        if last:
            refs = rest
        else:
            *r_refs, a, b, c, d, m, xn_ref, yn_ref, zs_ref = rest
            refs = (a, b, c, d, m)

        def keep(step, j, pack, meta):
            at, left, pb, hb = pack
            refs[0][step, j * slots : (j + 1) * slots] = at
            refs[1][step, :, j * 2 * slots : (j + 1) * 2 * slots] = left
            refs[2][step, j] = pb
            refs[3][step, j] = hb
            refs[4][step, :, j * slots : (j + 1) * slots] = meta

        first = [o_ref[1], o_ref[0], x_ref[0], x_ref[1], e_ref[0], e_ref[1]]
        packs = [terms(b, members) for b in first]
        for j in range(4):
            keep(0, j, packs[j + 1], first[j + 1][members:])
        second = [o_ref[2], x_ref[2], y_ref[...], e_ref[2]]
        for j in range(4):
            near = packs[j : j + 3]
            block = second[j]
            new = apply(
                block[:members],
                block[members + 2 : members + 3],
                jnp.concatenate([q[0] for q in near], axis=0),
                jnp.concatenate([q[1] for q in near], axis=1),
                [q[2] for q in near],
                [q[3] for q in near],
            )
            new = jnp.concatenate([new, block[members:]], axis=0)
            keep(1, j, terms(new, members), block[members:])
        if not last:
            wide = []
            for t in range(2):
                wide.append(jnp.concatenate([r_refs[t][0], r_refs[t][1]], axis=1))
                zs_ref[t] = wide[t][:members]

            def one(step, carry):
                new = [
                    apply(
                        zs_ref[t],
                        wide[t][members + 2 : members + 3],
                        *window(refs, step, t, slots),
                    )
                    for t in range(2)
                ]
                for t in range(2):
                    zs_ref[t] = new[t]
                return carry

            lax.fori_loop(0, 2, one, 0)
            for t in range(2):
                done = jnp.concatenate([zs_ref[t], wide[t][members:]], axis=0)
                xn_ref[t] = done[:, :slots]
                if t == 0:
                    xn_ref[2] = done[:, slots:]
                else:
                    yn_ref[...] = done[:, slots:]

    pack_shapes = (
        vmem((2, 4 * slots, WIDE), BF16),
        vmem((2, 2 * members, 8 * slots), BF16),
        vmem((2, 4, slots, slots), F32),
        vmem((2, 4, slots, slots), F32),
        vmem((2, META, 4 * slots), F32),
    )
    next_shapes = (vmem((3, full, slots), F32), vmem((full, slots), F32))
    return pl.pallas_call(
        crit,
        out_shape=pack_shapes if last else pack_shapes + next_shapes,
        scratch_shapes=() if last else (pltpu.VMEM((2, members, 2 * slots), F32),),
        compiler_params=pltpu.CompilerParams(vmem_limit_bytes=ROOM),
        name="crit",
    )


def run_steps(zs_ref, tpos, refs, t, slots):
    def one(step, carry):
        new = [
            apply(zs_ref[i], tpos[i], *window(refs, step, t, slots)) for i in range(len(tpos))
        ]
        for i in range(len(tpos)):
            zs_ref[i] = new[i]
        return carry

    lax.fori_loop(0, 2, one, 0)


def make_rows(members, slots, groups):
    full = members + META

    def rows(begin_ref, *all_refs):
        *refs, r_ref, n_ref, ro_ref, zs_ref = all_refs
        begin = begin_ref[0]

        def couple(c, carry):
            tpos = []
            for i in range(2):
                q = begin + 2 * c + i
                both = jnp.concatenate([ro_ref[q, 0], ro_ref[q, 1]], axis=1)
                zs_ref[i] = both[:members]
                tpos.append(both[members + 2 : members + 3])
            run_steps(zs_ref, tpos, refs, 0, slots)
            for i in range(2):
                q = begin + 2 * c + i
                for k in range(2):
                    ro_ref[q, k, :members] = zs_ref[i, :, k * slots : (k + 1) * slots]
            return carry

        lax.fori_loop(0, (groups - begin + 1) // 2, couple, 0)
        n_ref[...] = ro_ref[begin]

    smem = pl.BlockSpec(memory_space=pltpu.SMEM)
    rest = [pl.BlockSpec(memory_space=pltpu.VMEM)] * 6
    return pl.pallas_call(
        rows,
        in_specs=[smem] + rest,
        out_shape=(vmem((2, full, slots), F32), vmem((groups + 1, 2, full, slots), F32)),
        input_output_aliases={6: 1},
        scratch_shapes=(pltpu.VMEM((2, members, 2 * slots), F32),),
        compiler_params=pltpu.CompilerParams(vmem_limit_bytes=ROOM),
        name="rows",
    )


def make_cells(members, slots, cells, steps):
    part = min(cells, 2 * slots)
    chains = min(4, cells // part)
    span = 3 * slots

    def update(*all_refs):
        at_ref, left_ref, meta_ref, tri_ref, cpos_ref, s_ref, so_ref, *work = all_refs
        atc_ref, leftc_ref, pbc_ref, hbc_ref, zst_ref = work
        now_ref = s_ref if len(steps) == 1 else so_ref
        if len(steps) > 1:
            so_ref[...] = s_ref[...]

        def one_step(step):
            meta = meta_ref[step, :, :span]
            pos, half, live = meta[2:3], meta[3:4], meta[4:5]
            begin, end = cpos_ref[:, :1], cpos_ref[:, cells - 1 :]
            near = jnp.where((pos + half > begin) & (pos - half < end), live, 0.0)
            before = jnp.dot(
                jnp.broadcast_to(near, (16, span)).astype(BF16),
                tri_ref[...],
                preferred_element_type=F32,
            )
            spot = jnp.where(near > 0.5, before[:1], -1.0)
            count = (jnp.sum(near).astype(jnp.int32) + (slots - 1)) // slots
            lefts = jnp.concatenate(
                [left_ref[step, :, 2 * t * slots : (2 * t + 1) * slots] for t in range(3)], axis=1
            )

            def pick(c):
                rank = lax.broadcasted_iota(jnp.int32, (slots, span), 0) + c * slots
                hot = jnp.where(rank.astype(F32) == spot, 1.0, 0.0).astype(BF16)
                got = jnp.dot(hot, at_ref[step, :span], preferred_element_type=F32)
                atc_ref[c] = got.astype(BF16)
                k = 3 * members
                where = got[:, k + 1 : k + 2] + got[:, k + 2 : k + 3] + got[:, k + 3 : k + 4]
                pbc_ref[c] = jnp.broadcast_to(where, (slots, slots))
                hbc_ref[c] = jnp.broadcast_to(got[:, k : k + 1], (slots, slots))
                inc = lax.dot_general(
                    lefts, hot, (((1,), (1,)), ((), ())), preferred_element_type=F32
                )
                high, low = inc[:members], inc[members:]
                leftc_ref[c] = jnp.concatenate(
                    [
                        jnp.concatenate([high, high], axis=1),
                        jnp.concatenate([low, jnp.zeros_like(low)], axis=1),
                    ],
                    axis=0,
                ).astype(BF16)

            def looped(body):
                def one(c, carry):
                    body(c)
                    return carry

                lax.fori_loop(0, count, one, 0)

            looped(pick)

            def cells_step(n, carry):
                ats = [
                    pl.ds(pl.multiple_of((chains * n + i) * part, part), part) for i in range(chains)
                ]
                for i, a in enumerate(ats):
                    z = now_ref[:, a]
                    zst_ref[i] = centered(z)
                    so_ref[:, a] = z

                def add(c):
                    more = [
                        change(
                            zst_ref[i], cpos_ref[:, a], atc_ref[c], leftc_ref[c], [pbc_ref[c]], [hbc_ref[c]]
                        )
                        for i, a in enumerate(ats)
                    ]
                    for i, a in enumerate(ats):
                        so_ref[:, a] = so_ref[:, a] + more[i]

                looped(add)
                return carry

            lax.fori_loop(0, cells // (chains * part), cells_step, 0)

        if len(steps) == 1:
            one_step(steps[0])
        else:
            lax.fori_loop(0, 2, lambda step, carry: (one_step(step), carry)[1], 0)

    return pl.pallas_call(
        update,
        out_shape=vmem((members, cells), F32),
        input_output_aliases={5: 0},
        scratch_shapes=(
            pltpu.VMEM((3, slots, WIDE), BF16),
            pltpu.VMEM((3, 2 * members, 2 * slots), BF16),
            pltpu.VMEM((3, slots, slots), F32),
            pltpu.VMEM((3, slots, slots), F32),
            pltpu.VMEM((chains, WIDE, part), BF16),
        ),
        compiler_params=pltpu.CompilerParams(vmem_limit_bytes=ROOM),
        name="cells",
    )


def on_device(state, obs_rows, obs_value, obs_noise, obs_cell, obs_class, obs_count):
    members, _, cells = state.shape
    slots = obs_rows.shape[3]
    nbatch = lax.axis_size("region")
    tiles = lax.axis_size("tile")
    chips = tiles // 2
    region_index = lax.axis_index("region")
    tile_index = lax.axis_index("tile")
    tile_width = cells * nbatch
    cell_pos = (
        tile_index * tile_width + region_index * cells + jnp.arange(cells, dtype=jnp.int32)
    ).astype(F32)[None]
    pos = (tile_index * tile_width + obs_cell[0, 0]).astype(F32)
    half = (tile_width / 4) * (obs_class[0, 0] + 2).astype(F32)
    live = (jnp.arange(slots, dtype=jnp.int32) < obs_count[0, 0]).astype(F32)
    zero = jnp.zeros_like(pos)
    block = jnp.concatenate(
        [
            obs_rows[0, :, 0, :],
            jnp.stack([obs_value[0, 0], obs_noise[0, 0], pos, half, live, zero, zero, zero]),
        ],
        axis=0,
    )
    own = lax.all_to_all(
        jnp.broadcast_to(block[None], (nbatch,) + block.shape), "region", 0, 0, tiled=True
    )
    partner = [(i, i ^ 1) for i in range(tiles)]
    across = []
    for z in range(chips):
        across += [(2 * z + 1, 2 * ((z + 1) % chips)), (2 * z, 2 * ((z - 1) % chips) + 1)]
    groups = nbatch // 2
    begun = min(nbatch, 4)
    other = lax.ppermute(own[:begun], "tile", partner)
    x = jnp.stack([own[0], other[0], own[1]])
    y = other[1]
    near = own[2:4]
    far = other[2:4]
    rest = jnp.concatenate([own, jnp.zeros_like(own[:2])]).reshape(groups + 1, 2, *block.shape)
    cells_now = state[:, 0, :]
    order = jnp.arange(3 * slots, dtype=jnp.int32)
    tri = (order[:, None] < order[None, :]).astype(BF16)

    def update(steps, packs, cells_now):
        at, left, _, _, meta = packs
        kernel = make_cells(members, slots, cells, steps)
        return kernel(*inside(at, left, meta, tri, cell_pos, cells_now))

    crit = make_crit(members, slots, False)
    rows = make_rows(members, slots, groups)

    def middle(g, carry):
        x, y, rest, cells_now, *packs = carry
        o = lax.ppermute(x, "tile", across)
        if g > 2:
            cells_now = update((0,), packs, cells_now)
            o, cells_now = lax.optimization_barrier((o, cells_now))
        near, rest = rows(jnp.full((1,), g + 1, jnp.int32), *inside(*packs, rest))
        o, near = lax.optimization_barrier((o, near))
        far = lax.ppermute(near, "tile", partner)
        e = lax.ppermute(o, "tile", partner)
        cells_now = update((1,) if g > 2 else (0, 1), packs, cells_now)
        e, far, cells_now = lax.optimization_barrier((e, far, cells_now))
        *packs, x, y = crit(*inside(x, y, o, e, near, far))
        return (x, y, rest, cells_now, *packs)

    o = lax.ppermute(x, "tile", across)
    e = lax.ppermute(o, "tile", partner)
    *packs, x, y = crit(*inside(x, y, o, e, near, far))
    carry = (x, y, rest, cells_now, *packs)
    for g in range(1, groups - 1):
        carry = middle(g, carry)
    x, y, rest, cells_now, *packs = carry
    o = lax.ppermute(x, "tile", across)
    cells_now = update((0,), packs, cells_now)
    o, cells_now = lax.optimization_barrier((o, cells_now))
    e = lax.ppermute(o, "tile", partner)
    cells_now = update((1,), packs, cells_now)
    e, cells_now = lax.optimization_barrier((e, cells_now))
    packs = make_crit(members, slots, True)(*inside(x, y, o, e))
    cells_now = update((0, 1), packs, cells_now)
    return cells_now[:, None, :]


def solution(mesh):
    placed = (
        P(None, "tile", "region"),
        P("region", None, "tile", None),
        P("region", "tile", None),
        P("region", "tile", None),
        P("region", "tile", None),
        P("region", "tile", None),
        P("region", "tile"),
    )
    return jax.shard_map(
        on_device, mesh=mesh, in_specs=placed, out_specs=P(None, "tile", "region"), check_vma=False
    )
```

```python
import jax
import jax.numpy as jnp
from jax import lax
from jax.experimental import pallas as pl
from jax.experimental.pallas import tpu as pltpu
from jax.sharding import PartitionSpec as P

EPSILON = 1e-06
META = 8
WIDE = 256
ROOM = 16 * 1024 * 1024
F32 = jnp.float32
BF16 = jnp.bfloat16


def split(x):
    hi = x.astype(BF16).astype(F32)
    return hi, x - hi


def terms(block, members):
    rows = block[:members]
    meta = block[members : members + META]
    val, noise, pos, half, live = (meta[i : i + 1] for i in range(5))
    mean = jnp.sum(rows, axis=0, keepdims=True) / members
    an = rows - mean
    var = jnp.sum(an * an, axis=0, keepdims=True) / (members - 1) + EPSILON
    post_var = 1.0 / (1.0 / var + 1.0 / noise)
    post_mean = post_var * (mean / var + val / noise)
    shift = jnp.where(live > 0.5, post_mean - mean, 0.0)
    factor = jnp.where(live > 0.5, jnp.sqrt(post_var / var) - 1.0, 0.0)
    scale = 1.0 / ((members - 1) * var * (half * half))
    slots = rows.shape[1]
    a_hi, a_lo = split(an * scale)
    p_hi, p_rest = split(pos)
    p_mid, p_lo = split(p_rest)
    stack = jnp.concatenate(
        [
            *(a_hi, a_hi, a_lo, half, p_hi, p_mid, p_lo, pos),
            jnp.zeros((WIDE - 3 * members - 5, slots), F32),
        ],
        axis=0,
    )
    turned = jnp.transpose(stack)
    at = turned.astype(BF16)
    pb = jnp.broadcast_to(turned[:, 3 * members + 4 : 3 * members + 5], (slots, slots))
    hb = jnp.broadcast_to(turned[:, 3 * members : 3 * members + 1], (slots, slots))
    inc = shift + factor * an
    i_hi, i_lo = split(inc)
    lower = jnp.concatenate([i_lo, jnp.zeros_like(i_lo)], axis=1)
    left = jnp.concatenate([jnp.concatenate([i_hi, i_hi], axis=1), lower], axis=0).astype(BF16)
    return at, left, pb, hb


def centered(z):
    members, n = z.shape
    zc = z - jnp.sum(z, axis=0, keepdims=True) / members
    z_hi, z_lo = split(zc)
    return jnp.concatenate(
        [z_hi, z_lo, z_hi, jnp.zeros((WIDE - 3 * members, n), F32)], axis=0
    ).astype(BF16)


def change(zst, tpos, at, left, pbs, hbs):
    n = zst.shape[1]
    cov = jnp.dot(at, zst, preferred_element_type=F32)
    gains = []
    slots = pbs[0].shape[0]
    for j in range(len(pbs)):
        reps = n // pbs[j].shape[1]
        pb = jnp.concatenate([pbs[j]] * reps, axis=1) if reps > 1 else pbs[j]
        hb = jnp.concatenate([hbs[j]] * reps, axis=1) if reps > 1 else hbs[j]
        m = jnp.maximum(hb - jnp.abs(tpos - pb), 0.0)
        g = m * (m * cov[j * slots : (j + 1) * slots])
        g_hi = g.astype(BF16)
        g_lo = (g - g_hi.astype(F32)).astype(BF16)
        gains += [g_hi, g_lo]
    acc = jnp.dot(left, jnp.concatenate(gains, axis=0), preferred_element_type=F32)
    members = left.shape[0] // 2
    return acc[:members] + acc[members:]


def apply(z, tpos, *sources):
    return z + change(centered(z), tpos, *sources)


def window(refs, step, t, slots):
    at_ref, left_ref, pb_ref, hb_ref, _ = refs
    return (
        at_ref[step, t * slots : (t + 3) * slots],
        left_ref[step, :, t * 2 * slots : (t + 3) * 2 * slots],
        [pb_ref[step, t + j] for j in range(3)],
        [hb_ref[step, t + j] for j in range(3)],
    )


def vmem(shape, dtype):
    return pltpu.VMEM(shape, dtype)


def inside(*arrays):
    return [pltpu.with_memory_space_constraint(a, pltpu.VMEM) for a in arrays]


def make_prepare(members, slots, nbatch, tile_width):
    full = members + META

    def prepare(start_ref, count_ref, rows_ref, val_ref, noise_ref, cell_ref, class_ref, b_ref):
        lane = lax.broadcasted_iota(jnp.int32, (1, slots), 1)
        meta = [
            val_ref[...],
            noise_ref[...],
            (cell_ref[...] + start_ref[0]).astype(F32),
            (tile_width / 4) * (class_ref[...] + 2).astype(F32),
            jnp.where(lane < count_ref[0, 0], 1.0, 0.0),
            jnp.zeros((META - 5, slots), F32),
        ]
        meta = jnp.concatenate(meta, axis=0)
        for b in range(nbatch):
            b_ref[b, :members] = rows_ref[...]
            b_ref[b, members:] = meta

    smem = pl.BlockSpec(memory_space=pltpu.SMEM)
    return pl.pallas_call(
        prepare,
        in_specs=[smem] * 2 + [pl.BlockSpec(memory_space=pltpu.VMEM)] * 5,
        out_shape=vmem((nbatch, full, slots), F32),
        compiler_params=pltpu.CompilerParams(vmem_limit_bytes=ROOM),
        name="prepare",
    )


def make_crit(members, slots, last):
    full = members + META

    def crit(x_ref, y_ref, o_ref, e_ref, *rest):
        if last:
            refs = rest
        else:
            *r_refs, a, b, c, d, m, xn_ref, yn_ref, zs_ref = rest
            refs = (a, b, c, d, m)

        def keep(step, j, pack, meta):
            at, left, pb, hb = pack
            refs[0][step, j * slots : (j + 1) * slots] = at
            refs[1][step, :, j * 2 * slots : (j + 1) * 2 * slots] = left
            refs[2][step, j] = pb
            refs[3][step, j] = hb
            refs[4][step, :, j * slots : (j + 1) * slots] = meta

        first = [o_ref[1], o_ref[0], x_ref[0], x_ref[1], e_ref[0], e_ref[1]]
        packs = [terms(b, members) for b in first]
        for j in range(4):
            keep(0, j, packs[j + 1], first[j + 1][members:])
        second = [o_ref[2], x_ref[2], y_ref[...], e_ref[2]]
        for j in range(4):
            near = packs[j : j + 3]
            block = second[j]
            new = apply(
                block[:members],
                block[members + 2 : members + 3],
                jnp.concatenate([q[0] for q in near], axis=0),
                jnp.concatenate([q[1] for q in near], axis=1),
                [q[2] for q in near],
                [q[3] for q in near],
            )
            new = jnp.concatenate([new, block[members:]], axis=0)
            keep(1, j, terms(new, members), block[members:])
        if not last:
            wide = []
            for t in range(2):
                wide.append(jnp.concatenate([r_refs[t][0], r_refs[t][1]], axis=1))
                zs_ref[t] = wide[t][:members]

            def one(step, carry):
                new = [
                    apply(
                        zs_ref[t],
                        wide[t][members + 2 : members + 3],
                        *window(refs, step, t, slots),
                    )
                    for t in range(2)
                ]
                for t in range(2):
                    zs_ref[t] = new[t]
                return carry

            lax.fori_loop(0, 2, one, 0)
            for t in range(2):
                done = jnp.concatenate([zs_ref[t], wide[t][members:]], axis=0)
                xn_ref[t] = done[:, :slots]
                if t == 0:
                    xn_ref[2] = done[:, slots:]
                else:
                    yn_ref[...] = done[:, slots:]

    pack_shapes = (
        vmem((2, 4 * slots, WIDE), BF16),
        vmem((2, 2 * members, 8 * slots), BF16),
        vmem((2, 4, slots, slots), F32),
        vmem((2, 4, slots, slots), F32),
        vmem((2, META, 4 * slots), F32),
    )
    next_shapes = (vmem((3, full, slots), F32), vmem((full, slots), F32))
    return pl.pallas_call(
        crit,
        out_shape=pack_shapes if last else pack_shapes + next_shapes,
        scratch_shapes=() if last else (pltpu.VMEM((2, members, 2 * slots), F32),),
        compiler_params=pltpu.CompilerParams(vmem_limit_bytes=ROOM),
        name="crit",
    )


def run_steps(zs_ref, tpos, refs, t, slots):
    def one(step, carry):
        new = [
            apply(zs_ref[i], tpos[i], *window(refs, step, t, slots)) for i in range(len(tpos))
        ]
        for i in range(len(tpos)):
            zs_ref[i] = new[i]
        return carry

    lax.fori_loop(0, 2, one, 0)


def make_rows(members, slots, groups, abreast):
    full = members + META

    def rows(begin_ref, *all_refs):
        *refs, r_ref, n_ref, ro_ref, zs_ref = all_refs
        begin = begin_ref[0]

        def several(c, carry):
            spots = [jnp.minimum(begin + abreast * c + i, groups - 1) for i in range(abreast)]
            tpos = []
            for i, q in enumerate(spots):
                both = jnp.concatenate([ro_ref[q, 0], ro_ref[q, 1]], axis=1)
                zs_ref[i] = both[:members]
                tpos.append(both[members + 2 : members + 3])
            run_steps(zs_ref, tpos, refs, 0, slots)
            for i, q in enumerate(spots):
                for k in range(2):
                    ro_ref[q, k, :members] = zs_ref[i, :, k * slots : (k + 1) * slots]
            return carry

        lax.fori_loop(0, (groups - begin + abreast - 1) // abreast, several, 0)
        n_ref[...] = ro_ref[begin]

    smem = pl.BlockSpec(memory_space=pltpu.SMEM)
    rest = [pl.BlockSpec(memory_space=pltpu.VMEM)] * 6
    return pl.pallas_call(
        rows,
        in_specs=[smem] + rest,
        out_shape=(vmem((2, full, slots), F32), vmem((groups, 2, full, slots), F32)),
        input_output_aliases={6: 1},
        scratch_shapes=(pltpu.VMEM((abreast, members, 2 * slots), F32),),
        compiler_params=pltpu.CompilerParams(vmem_limit_bytes=ROOM),
        name="rows",
    )


def make_cells(members, slots, cells, steps):
    part = min(cells, 2 * slots)
    chains = min(4, cells // part)
    span = 3 * slots

    def update(*all_refs):
        at_ref, left_ref, meta_ref, tri_ref, cpos_ref, s_ref, so_ref, *work = all_refs
        atc_ref, leftc_ref, pbc_ref, hbc_ref, zst_ref = work
        now_ref = s_ref if len(steps) == 1 else so_ref
        if len(steps) > 1:
            so_ref[...] = s_ref[...]

        def one_step(step):
            meta = meta_ref[step, :, :span]
            pos, half, live = meta[2:3], meta[3:4], meta[4:5]
            begin, end = cpos_ref[:, :1], cpos_ref[:, cells - 1 :]
            near = jnp.where((pos + half > begin) & (pos - half < end), live, 0.0)
            before = jnp.dot(
                jnp.broadcast_to(near, (16, span)).astype(BF16),
                tri_ref[...],
                preferred_element_type=F32,
            )
            spot = jnp.where(near > 0.5, before[:1], -1.0)
            count = (jnp.sum(near).astype(jnp.int32) + (slots - 1)) // slots
            lefts = jnp.concatenate(
                [left_ref[step, :, 2 * t * slots : (2 * t + 1) * slots] for t in range(3)], axis=1
            )

            def pick(c):
                rank = lax.broadcasted_iota(jnp.int32, (slots, span), 0) + c * slots
                hot = jnp.where(rank.astype(F32) == spot, 1.0, 0.0).astype(BF16)
                got = jnp.dot(hot, at_ref[step, :span], preferred_element_type=F32)
                atc_ref[c] = got.astype(BF16)
                k = 3 * members
                where = got[:, k + 1 : k + 2] + got[:, k + 2 : k + 3] + got[:, k + 3 : k + 4]
                pbc_ref[c] = jnp.broadcast_to(where, (slots, slots))
                hbc_ref[c] = jnp.broadcast_to(got[:, k : k + 1], (slots, slots))
                inc = lax.dot_general(
                    lefts, hot, (((1,), (1,)), ((), ())), preferred_element_type=F32
                )
                high, low = inc[:members], inc[members:]
                leftc_ref[c] = jnp.concatenate(
                    [
                        jnp.concatenate([high, high], axis=1),
                        jnp.concatenate([low, jnp.zeros_like(low)], axis=1),
                    ],
                    axis=0,
                ).astype(BF16)

            def looped(body):
                def one(c, carry):
                    body(c)
                    return carry

                lax.fori_loop(0, count, one, 0)

            looped(pick)

            def cells_step(n, carry):
                ats = [
                    pl.ds(pl.multiple_of((chains * n + i) * part, part), part) for i in range(chains)
                ]
                for i, a in enumerate(ats):
                    z = now_ref[:, a]
                    zst_ref[i] = centered(z)
                    so_ref[:, a] = z

                def add(c):
                    more = [
                        change(
                            zst_ref[i], cpos_ref[:, a], atc_ref[c], leftc_ref[c], [pbc_ref[c]], [hbc_ref[c]]
                        )
                        for i, a in enumerate(ats)
                    ]
                    for i, a in enumerate(ats):
                        so_ref[:, a] = so_ref[:, a] + more[i]

                looped(add)
                return carry

            lax.fori_loop(0, cells // (chains * part), cells_step, 0)

        if len(steps) == 1:
            one_step(steps[0])
        else:
            lax.fori_loop(0, 2, lambda step, carry: (one_step(step), carry)[1], 0)

    return pl.pallas_call(
        update,
        out_shape=vmem((members, cells), F32),
        input_output_aliases={5: 0},
        scratch_shapes=(
            pltpu.VMEM((3, slots, WIDE), BF16),
            pltpu.VMEM((3, 2 * members, 2 * slots), BF16),
            pltpu.VMEM((3, slots, slots), F32),
            pltpu.VMEM((3, slots, slots), F32),
            pltpu.VMEM((chains, WIDE, part), BF16),
        ),
        compiler_params=pltpu.CompilerParams(vmem_limit_bytes=ROOM),
        name="cells",
    )


def on_device(state, obs_rows, obs_value, obs_noise, obs_cell, obs_class, obs_count):
    members, _, cells = state.shape
    slots = obs_rows.shape[3]
    nbatch = lax.axis_size("region")
    tiles = lax.axis_size("tile")
    chips = tiles // 2
    region_index = lax.axis_index("region")
    tile_index = lax.axis_index("tile")
    tile_width = cells * nbatch
    cell_pos = (
        tile_index * tile_width + region_index * cells + jnp.arange(cells, dtype=jnp.int32)
    ).astype(F32)[None]
    prepare = make_prepare(members, slots, nbatch, tile_width)
    copies = prepare(
        jnp.full((1,), tile_index * tile_width, jnp.int32),
        obs_count,
        *(obs_rows[0, :, 0, :], obs_value[0], obs_noise[0], obs_cell[0], obs_class[0]),
    )
    own = lax.all_to_all(copies, "region", 0, 0, tiled=True)
    block = own[0]
    partner = [(i, i ^ 1) for i in range(tiles)]
    across = []
    for z in range(chips):
        across += [(2 * z + 1, 2 * ((z + 1) % chips)), (2 * z, 2 * ((z - 1) % chips) + 1)]
    groups = nbatch // 2
    begun = min(nbatch, 4)
    other = lax.ppermute(own[:begun], "tile", partner)
    x = jnp.stack([own[0], other[0], own[1]])
    y = other[1]
    near = own[2:4]
    far = other[2:4]
    rest = own.reshape(groups, 2, *block.shape)
    cells_now = state[:, 0, :]
    order = jnp.arange(3 * slots, dtype=jnp.int32)
    tri = (order[:, None] < order[None, :]).astype(BF16)

    def update(steps, packs, cells_now):
        at, left, _, _, meta = packs
        kernel = make_cells(members, slots, cells, steps)
        return kernel(*inside(at, left, meta, tri, cell_pos, cells_now))

    crit = make_crit(members, slots, False)

    def middle(g, carry):
        x, y, rest, cells_now, *packs = carry
        o = lax.ppermute(x, "tile", across)
        if g > 2:
            cells_now = update((0,), packs, cells_now)
            o, cells_now = lax.optimization_barrier((o, cells_now))
        left = groups - g - 1
        rows = make_rows(members, slots, groups, left if left < 4 else 2 + left // 5)
        near, rest = rows(jnp.full((1,), g + 1, jnp.int32), *inside(*packs, rest))
        o, near = lax.optimization_barrier((o, near))
        far = lax.ppermute(near, "tile", partner)
        e = lax.ppermute(o, "tile", partner)
        cells_now = update((1,) if g > 2 else (0, 1), packs, cells_now)
        e, far, cells_now = lax.optimization_barrier((e, far, cells_now))
        *packs, x, y = crit(*inside(x, y, o, e, near, far))
        return (x, y, rest, cells_now, *packs)

    o = lax.ppermute(x, "tile", across)
    e = lax.ppermute(o, "tile", partner)
    *packs, x, y = crit(*inside(x, y, o, e, near, far))
    carry = (x, y, rest, cells_now, *packs)
    for g in range(1, groups - 1):
        carry = middle(g, carry)
    x, y, rest, cells_now, *packs = carry
    o = lax.ppermute(x, "tile", across)
    cells_now = update((0,), packs, cells_now)
    o, cells_now = lax.optimization_barrier((o, cells_now))
    e = lax.ppermute(o, "tile", partner)
    cells_now = update((1,), packs, cells_now)
    e, cells_now = lax.optimization_barrier((e, cells_now))
    packs = make_crit(members, slots, True)(*inside(x, y, o, e))
    cells_now = update((0, 1), packs, cells_now)
    return cells_now[:, None, :]


def solution(mesh):
    placed = (
        P(None, "tile", "region"),
        P("region", None, "tile", None),
        P("region", "tile", None),
        P("region", "tile", None),
        P("region", "tile", None),
        P("region", "tile", None),
        P("region", "tile"),
    )
    return jax.shard_map(
        on_device, mesh=mesh, in_specs=placed, out_specs=P(None, "tile", "region"), check_vma=False
    )
```
